512 devices in a mesh: ctx: 64 (over x, z), qg: 8 (over y, core).
Axes of the slice: x: 4, y: 4, z: 16, core: 2. Of those that a mesh axis runs over, the one named last changes fastest.
Arguments:
- queries: bfloat16 [32, 32, 768], P('qg'), may hold values from -9 to 9
- documents: bfloat16 [16, 32768, 768], P('qg', 'ctx'), may hold values from -2.5 to 2.5
- candidates: int32 [32, 4], replicated, may hold values from 0 to 15, all different within a row
Outputs:
- loss: float32 [], replicated
- grad_queries: bfloat16 [32, 32, 768], P('qg')
- grad_documents: bfloat16 [16, 32768, 768], P('qg', 'ctx')
The draws below stay inside these ranges and needn't reach their ends.
Inputs may be any that keep to these rules, and one draw needn't show every extreme that they name: `candidates`: each row names 4 different documents; every document is named by some row.
All inputs are finite; a program needn't handle non-finite values.
Results may differ from the reference program's by a relative error of at most 0.006.
Values may be sent and summed in bfloat16 or wider, within the bound.
No kernel may reach another device: no remote copies, remote signals or barrier semaphores. Data moves between devices by JAX's collectives and lax.ppermute only.
A program may use at most 64 MiB of HBM per device.

```python
import jax
import jax.numpy as jnp
from jax import lax

MODEL_WIDTH = 768
QT = 32
CANDIDATE_DOCS = 4
L = 32768
QUERY_COUNT = 32
ND = 16


def draw_queries(key, part):
    base = jnp.clip(jax.random.normal(jax.random.fold_in(key, 11), (QUERY_COUNT, QT, MODEL_WIDTH), jnp.float32), -6.0, 6.0) * MODEL_WIDTH ** (-0.25)
    return base.astype(jnp.bfloat16)


def draw_documents(key, part):
    base = jnp.clip(jax.random.normal(jax.random.fold_in(key, 21), (ND, L, MODEL_WIDTH), jnp.float32), -6.0, 6.0) * MODEL_WIDTH ** (-0.25)
    return base.astype(jnp.bfloat16)


def choose_distinct(key, rows, count, top, lift):
    sequence = jax.random.permutation(jax.random.fold_in(key, 1), count)
    boost = sequence
    for power in range(3):
        boost = boost * boost // count
    boost = boost * lift // count
    tickets = jax.random.randint(jax.random.fold_in(key, 2), (rows, count), 0, 4096) + boost
    holders = jax.random.permutation(jax.random.fold_in(key, 3), rows)[jnp.arange(count) % rows]
    tickets = jnp.where(jnp.arange(rows)[:, None] == holders[None, :], 1 << 14, tickets)
    merit = tickets * count + jnp.arange(count)
    return lax.top_k(merit.astype(jnp.int32), top)[1].astype(jnp.int32)


def setup_inputs(seed: int = 0) -> dict:
    arg_keys = jax.random.split(jax.random.key(seed), 4)
    return {
        "queries": draw_queries(jax.random.fold_in(arg_keys[3], 71), 0),
        "documents": draw_documents(jax.random.fold_in(arg_keys[3], 71), 0),
        "candidates": choose_distinct(arg_keys[2], QUERY_COUNT, ND, CANDIDATE_DOCS, 4096),
    }


sharpness_factor = 2.0
loss_scale = 1024.0


def reference(queries, documents, candidates):
    query_ids = jnp.repeat(jnp.arange(QUERY_COUNT, dtype=jnp.int32), CANDIDATE_DOCS)
    doc_ids = candidates.reshape(-1).astype(jnp.int32)

    def forward(pair_ids):
        query_index, document_index = pair_ids
        candidate_logits = sharpness_factor * lax.dot_general(queries[query_index], documents[document_index], (((1,), (1,)), ((), ())), preferred_element_type=jnp.float32)
        return candidate_logits, jax.nn.logsumexp(candidate_logits, axis=1)

    logits_all, log_partition = lax.map(forward, (query_ids, doc_ids))
    query_document_pair = (jnp.sum(log_partition, axis=1) / sharpness_factor).reshape(QUERY_COUNT, CANDIDATE_DOCS)
    total = jax.nn.logsumexp(query_document_pair, axis=1)
    loss = jnp.mean(total - query_document_pair[:, 0])
    first = (jnp.arange(CANDIDATE_DOCS) == 0).astype(jnp.float32)
    dz = (loss_scale / QUERY_COUNT) * (jnp.exp(query_document_pair - total[:, None]) - first[None, :])

    def backward(carry, item):
        grad_q, grad_d = carry
        query_index, document_index, candidate_logits, norm, weight = item
        weighted = (weight * jnp.exp(candidate_logits - norm[:, None])).astype(jnp.bfloat16)
        grad_q = grad_q.at[query_index].add(jnp.dot(weighted, documents[document_index], preferred_element_type=jnp.float32))
        grad_d = grad_d.at[document_index].add(lax.dot_general(weighted, queries[query_index], (((0,), (0,)), ((), ())), preferred_element_type=jnp.float32))
        return (grad_q, grad_d), None

    start = (jnp.zeros((QUERY_COUNT, QT, MODEL_WIDTH), jnp.float32), jnp.zeros((ND, L, MODEL_WIDTH), jnp.float32))
    (grad_q, grad_d), unused = lax.scan(backward, start, (query_ids, doc_ids, logits_all, log_partition, dz.reshape(-1)))
    return loss, grad_q.astype(jnp.bfloat16), grad_d.astype(jnp.bfloat16)
```

```python
import jax
import jax.numpy as jnp
from jax import lax
from jax.sharding import Mesh
from jax.sharding import PartitionSpec as P

QG = ("y", "c")
CTX = ("x", "z")

sharpness_factor = 2.0
loss_scale = 1024.0


def copy_for_each(x, axis):
    copies = jnp.broadcast_to(x, (lax.axis_size(axis), *x.shape))
    return lax.all_to_all(copies, axis, split_axis=0, concat_axis=0, tiled=True)


def other_core(x):
    return lax.ppermute(x, "c", [(0, 1), (1, 0)])


def per_device(queries, documents, candidates):
    local_docs, doc_len, width = documents.shape
    per_group, query_len, _ = queries.shape
    slots = candidates.shape[1]
    rows_of_y = lax.axis_size("y")
    groups = lax.axis_size(QG)
    total_queries = per_group * groups
    total_rows = total_queries * query_len
    half = total_queries // 2
    core = lax.axis_index("c")

    def swap_order(t):
        pairs = t.reshape(rows_of_y, 2, per_group, *t.shape[1:])
        flip = jnp.where(core == 0, pairs, pairs[:, ::-1])
        return jnp.moveaxis(flip, 1, 0).reshape(t.shape)

    def swap_back(t):
        pairs = t.reshape(2, rows_of_y, per_group, *t.shape[1:])
        flip = jnp.where(core == 0, pairs, pairs[::-1])
        return jnp.moveaxis(flip, 0, 1).reshape(t.shape)

    own = copy_for_each(queries, "y").reshape(half * query_len, width)
    rows = jnp.concatenate([own, other_core(own)])

    logits = sharpness_factor * lax.dot_general(
        rows, documents, (((1,), (2,)), ((), ())), preferred_element_type=jnp.float32
    )
    peak = jnp.max(logits, axis=2)
    mass = jnp.sum(jnp.exp(logits - peak[:, :, None]), axis=2)
    local_lse = (peak + jnp.log(mass)).T.reshape(-1, 128)

    everywhere = copy_for_each(local_lse, CTX)
    top = jnp.max(everywhere, axis=0)
    lse = top + jnp.log(jnp.sum(jnp.exp(everywhere - top[None]), axis=0))
    lse = lse.reshape(local_docs, total_queries, query_len)

    scores = jnp.sum(lse, axis=2) / sharpness_factor
    scores = copy_for_each(swap_back(scores.T).T, QG).reshape(-1, total_queries)
    all_docs = scores.shape[0]
    picks = candidates[:, :, None] == jnp.arange(all_docs, dtype=jnp.int32)[None, None, :]
    pair = jnp.sum(jnp.where(picks, scores.T[:, None, :], 0.0), axis=2)
    highest = jnp.max(pair, axis=1)
    total = highest + jnp.log(jnp.sum(jnp.exp(pair - highest[:, None]), axis=1))
    loss = jnp.mean(total - pair[:, 0])
    first = (jnp.arange(slots) == 0).astype(jnp.float32)
    dz = loss_scale / total_queries * (jnp.exp(pair - total[:, None]) - first[None, :])
    group = lax.axis_index(QG)
    doc_ids = group * local_docs + jnp.arange(local_docs, dtype=jnp.int32)
    owned = candidates[:, :, None] == doc_ids[None, None, :]
    weights = swap_order(jnp.sum(jnp.where(owned, dz[:, :, None], 0.0), axis=1))
    row_weight = jnp.repeat(weights, query_len, axis=0)
    norm = lse.reshape(local_docs, total_rows).T

    weighted = (row_weight[:, :, None] * jnp.exp(logits - norm[:, :, None])).astype(jnp.bfloat16)
    grad_rows = lax.dot_general(
        weighted, documents, (((1, 2), (0, 1)), ((), ())), preferred_element_type=jnp.float32
    )
    grad_docs = lax.dot_general(
        weighted, rows, (((0,), (0,)), ((), ())), preferred_element_type=jnp.float32
    ).astype(jnp.bfloat16)

    mine, theirs = grad_rows[: total_rows // 2], grad_rows[total_rows // 2 :]
    chip = mine + other_core(theirs.astype(jnp.bfloat16)).astype(jnp.float32)
    tiles = chip.reshape(rows_of_y, -1, width).astype(jnp.bfloat16)
    arrived = lax.all_to_all(tiles, "y", split_axis=0, concat_axis=0, tiled=True)
    summed = jnp.sum(arrived.astype(jnp.float32), axis=0)
    tiles = summed.reshape(lax.axis_size(CTX), -1, width).astype(jnp.bfloat16)
    arrived = lax.all_to_all(tiles, CTX, split_axis=0, concat_axis=0, tiled=True)
    part = jnp.sum(arrived.astype(jnp.float32), axis=0).astype(jnp.bfloat16)
    grad_q = copy_for_each(part, CTX).reshape(queries.shape)
    return loss, grad_q, grad_docs


def solution(mesh):
    finer = Mesh(mesh.devices.reshape(4, 16, 4, 2), ("x", "z", "y", "c"))
    in_specs = (P(QG, None, None), P(QG, CTX, None), P())
    out_specs = (P(), P(QG, None, None), P(QG, CTX, None))
    return jax.shard_map(
        per_device, mesh=finer, in_specs=in_specs, out_specs=out_specs, check_vma=False
    )
```

```python
import jax
import jax.numpy as jnp
from jax import lax
from jax.sharding import Mesh
from jax.sharding import PartitionSpec as P

QG = ("y", "c")
CTX = ("x", "z")

sharpness_factor = 2.0
loss_scale = 1024.0


def copy_for_each(x, axis):
    copies = jnp.broadcast_to(x, (lax.axis_size(axis), *x.shape))
    return lax.all_to_all(copies, axis, split_axis=0, concat_axis=0, tiled=True)


def other_core(x):
    return lax.ppermute(x, "c", [(0, 1), (1, 0)])


def log_of_sum(x):
    top = jnp.max(x, axis=0)
    return top + jnp.log(jnp.sum(jnp.exp(x - top[None]), axis=0))


def sent_and_summed(x, axis):
    tiles = x.astype(jnp.bfloat16).reshape(lax.axis_size(axis), -1, x.shape[-1])
    arrived = lax.all_to_all(tiles, axis, split_axis=0, concat_axis=0, tiled=True)
    return jnp.sum(arrived.astype(jnp.float32), axis=0)


def per_device(queries, documents, candidates):
    local_docs, doc_len, width = documents.shape
    per_group, query_len, _ = queries.shape
    slots = candidates.shape[1]
    rows_of_y = lax.axis_size("y")
    groups = lax.axis_size(QG)
    total_queries = per_group * groups
    half_rows = total_queries * query_len // 2
    core = lax.axis_index("c")

    def swap_order(t):
        pairs = t.reshape(rows_of_y, 2, per_group, *t.shape[1:])
        flip = jnp.where(core == 0, pairs, pairs[:, ::-1])
        return jnp.moveaxis(flip, 1, 0).reshape(t.shape)

    def swap_back(t):
        pairs = t.reshape(2, rows_of_y, per_group, *t.shape[1:])
        flip = jnp.where(core == 0, pairs, pairs[::-1])
        return jnp.moveaxis(flip, 0, 1).reshape(t.shape)

    own = copy_for_each(queries, "y").reshape(half_rows, width)
    halves = [own, other_core(own)]

    logits, local_lse = [], []
    for rows in halves:
        part = sharpness_factor * lax.dot_general(
            rows, documents, (((1,), (2,)), ((), ())), preferred_element_type=jnp.float32
        )
        peak = jnp.max(part, axis=2)
        mass = jnp.sum(jnp.exp(part - peak[:, :, None]), axis=2)
        logits.append(part)
        local_lse.append(peak + jnp.log(mass))

    lse = jnp.concatenate(local_lse).T.reshape(-1, 128)
    lse = log_of_sum(copy_for_each(lse, "x"))
    lse = log_of_sum(copy_for_each(lse, "z"))
    lse, candidates = lax.optimization_barrier((lse, candidates))
    lse = lse.reshape(local_docs, total_queries, query_len)

    scores = jnp.sum(lse, axis=2) / sharpness_factor
    scores = copy_for_each(swap_back(scores.T).T, QG).reshape(-1, total_queries)
    all_docs = scores.shape[0]
    picks = candidates[:, :, None] == jnp.arange(all_docs, dtype=jnp.int32)[None, None, :]
    pair = jnp.sum(jnp.where(picks, scores.T[:, None, :], 0.0), axis=2)
    highest = jnp.max(pair, axis=1)
    total = highest + jnp.log(jnp.sum(jnp.exp(pair - highest[:, None]), axis=1))
    loss = jnp.mean(total - pair[:, 0])
    first = (jnp.arange(slots) == 0).astype(jnp.float32)
    dz = loss_scale / total_queries * (jnp.exp(pair - total[:, None]) - first[None, :])
    group = lax.axis_index(QG)
    doc_ids = group * local_docs + jnp.arange(local_docs, dtype=jnp.int32)
    owned = candidates[:, :, None] == doc_ids[None, None, :]
    weights = swap_order(jnp.sum(jnp.where(owned, dz[:, :, None], 0.0), axis=1))
    row_weight = jnp.repeat(weights, query_len, axis=0)
    norm = lse.reshape(local_docs, -1).T

    def weighted_half(k):
        at = slice(k * half_rows, (k + 1) * half_rows)
        prob = jnp.exp(logits[k] - norm[at, :, None])
        return (row_weight[at, :, None] * prob).astype(jnp.bfloat16)

    def grad_of_rows(weighted):
        return lax.dot_general(
            weighted, documents, (((1, 2), (0, 1)), ((), ())), preferred_element_type=jnp.float32
        )

    weighted = [weighted_half(0), weighted_half(1)]
    received = other_core(grad_of_rows(weighted[1]).astype(jnp.bfloat16))
    chip = grad_of_rows(weighted[0]) + received.astype(jnp.float32)
    summed = sent_and_summed(chip, ("y", "x"))
    part = sent_and_summed(summed, "z").astype(jnp.bfloat16)
    grad_q = copy_for_each(part, CTX).reshape(queries.shape)
    grad_docs = sum(
        lax.dot_general(
            weighted[k], halves[k], (((0,), (0,)), ((), ())), preferred_element_type=jnp.float32
        )
        for k in range(2)
    ).astype(jnp.bfloat16)
    return loss, grad_q, grad_docs


def solution(mesh):
    finer = Mesh(mesh.devices.reshape(4, 16, 4, 2), ("x", "z", "y", "c"))
    in_specs = (P(QG, None, None), P(QG, CTX, None), P())
    out_specs = (P(), P(QG, None, None), P(QG, CTX, None))
    return jax.shard_map(
        per_device, mesh=finer, in_specs=in_specs, out_specs=out_specs, check_vma=False
    )
```

```python
import jax
import jax.numpy as jnp
from jax import lax
from jax.sharding import Mesh
from jax.sharding import PartitionSpec as P

QG = ("y", "c")
CTX = ("x", "h", "l")

sharpness_factor = 2.0
loss_scale = 1024.0


def copy_for_each(x, axis):
    copies = jnp.broadcast_to(x, (lax.axis_size(axis), *x.shape))
    return lax.all_to_all(copies, axis, split_axis=0, concat_axis=0, tiled=True)


def other_core(x):
    return lax.ppermute(x, "c", [(0, 1), (1, 0)])


def log_of_sum(x):
    top = jnp.max(x, axis=0)
    return top + jnp.log(jnp.sum(jnp.exp(x - top[None]), axis=0))


def sent_and_summed(x, axis):
    tiles = x.astype(jnp.bfloat16).reshape(lax.axis_size(axis), -1, x.shape[-1])
    arrived = lax.all_to_all(tiles, axis, split_axis=0, concat_axis=0, tiled=True)
    return jnp.sum(arrived.astype(jnp.float32), axis=0)


def per_device(queries, documents, candidates):
    local_docs, doc_len, width = documents.shape
    per_group, query_len, _ = queries.shape
    slots = candidates.shape[1]
    rows_of_y = lax.axis_size("y")
    groups = lax.axis_size(QG)
    total_queries = per_group * groups
    half_rows = total_queries * query_len // 2
    core = lax.axis_index("c")

    own = copy_for_each(queries, "y").reshape(half_rows, width)
    halves = [own, other_core(own)]

    def scored(rows):
        return sharpness_factor * lax.dot_general(
            rows, documents, (((1,), (2,)), ((), ())), preferred_element_type=jnp.float32
        )

    local_lse = []
    for rows in halves:
        part = scored(rows)
        peak = jnp.max(part, axis=2)
        mass = jnp.sum(jnp.exp(part - peak[:, :, None]), axis=2)
        local_lse.append(peak + jnp.log(mass))

    own_order = jnp.concatenate(local_lse).T.reshape(local_docs, 2, -1, 128)
    lse = jnp.where(core == 0, own_order, own_order[:, ::-1]).reshape(-1, 128)
    lse = log_of_sum(copy_for_each(lse, ("h", "l")))
    everyone = copy_for_each(lse, ("x", *QG))
    lse = log_of_sum(everyone.reshape(lax.axis_size("x"), -1, 128))
    lse, candidates, core, group = lax.optimization_barrier(
        (lse, candidates, core, lax.axis_index(QG))
    )

    all_docs = groups * local_docs
    scores = jnp.sum(lse.reshape(all_docs, total_queries, query_len), axis=2) / sharpness_factor
    by_core = candidates.reshape(rows_of_y, 2, per_group, slots).swapaxes(0, 1)
    by_core = by_core.reshape(total_queries, slots)
    picks = by_core[:, :, None] == jnp.arange(all_docs, dtype=jnp.int32)[None, None, :]
    pair = jnp.sum(jnp.where(picks, scores.T[:, None, :], 0.0), axis=2)
    highest = jnp.max(pair, axis=1, keepdims=True)
    total = highest + jnp.log(jnp.sum(jnp.exp(pair - highest), axis=1, keepdims=True))
    first = lax.broadcasted_iota(jnp.int32, pair.shape, 1) == 0
    dz = loss_scale / total_queries * (jnp.exp(pair - total) - jnp.where(first, 1.0, 0.0))
    owned = by_core[:, :, None] - group * local_docs == jnp.arange(local_docs, dtype=jnp.int32)
    weights = jnp.sum(jnp.where(owned, dz[:, :, None], 0.0), axis=1).reshape(2, -1, local_docs)
    weights = jnp.where(core == 0, weights, weights[::-1]).reshape(total_queries, local_docs)
    row_weight = jnp.repeat(weights, query_len, axis=0)
    mine = lax.dynamic_slice_in_dim(lse, group * len(own_order.reshape(-1, 128)), len(lse) // groups)
    mine = mine.reshape(own_order.shape)
    norm = jnp.where(core == 0, mine, mine[:, ::-1]).reshape(local_docs, -1).T

    def weighted_half(k):
        at = slice(k * half_rows, (k + 1) * half_rows)
        rows, this_norm, this_weight = lax.optimization_barrier(
            (halves[k], norm[at], row_weight[at])
        )
        prob = jnp.exp(scored(rows) - this_norm[:, :, None])
        return lax.optimization_barrier((this_weight[:, :, None] * prob).astype(jnp.bfloat16))

    def grad_of_rows(weighted):
        return lax.dot_general(
            weighted, documents, (((1, 2), (0, 1)), ((), ())), preferred_element_type=jnp.float32
        )

    theirs = weighted_half(1)
    received = other_core(grad_of_rows(theirs).astype(jnp.bfloat16))
    ours = weighted_half(0)
    chip = lax.optimization_barrier(grad_of_rows(ours)) + received.astype(jnp.float32)
    summed = sent_and_summed(chip, ("y", "x"))
    part = sent_and_summed(summed, ("h", "l")).astype(jnp.bfloat16)
    part, total, pair = lax.optimization_barrier((part, total, pair))
    loss = jnp.mean(total - pair[:, :1])
    grad_q = copy_for_each(part, CTX).reshape(queries.shape)
    grad_docs = sum(
        lax.dot_general(w, rows, (((0,), (0,)), ((), ())), preferred_element_type=jnp.float32)
        for w, rows in zip((ours, theirs), halves)
    ).astype(jnp.bfloat16)
    return loss, grad_q, grad_docs


def solution(mesh):
    finer = Mesh(mesh.devices.reshape(4, 4, 4, 4, 2), ("x", "h", "l", "y", "c"))
    in_specs = (P(QG, None, None), P(QG, CTX, None), P())
    out_specs = (P(), P(QG, None, None), P(QG, CTX, None))
    return jax.shard_map(
        per_device, mesh=finer, in_specs=in_specs, out_specs=out_specs, check_vma=False
    )
```

```python
import jax
import jax.numpy as jnp
from jax import lax
from jax.sharding import Mesh
from jax.sharding import PartitionSpec as P

QG = ("y", "c")
CTX = ("x", "h", "l")

sharpness_factor = 2.0
loss_scale = 1024.0


def copy_for_each(x, axis):
    copies = jnp.broadcast_to(x, (lax.axis_size(axis), *x.shape))
    return lax.all_to_all(copies, axis, split_axis=0, concat_axis=0, tiled=True)


def other_core(x):
    return lax.ppermute(x, "c", [(0, 1), (1, 0)])


def log_of_sum(x):
    top = jnp.max(x, axis=0)
    return top + jnp.log(jnp.sum(jnp.exp(x - top[None]), axis=0))


def sent_and_summed(x, axis):
    tiles = x.astype(jnp.bfloat16).reshape(lax.axis_size(axis), -1, x.shape[-1])
    arrived = lax.all_to_all(tiles, axis, split_axis=0, concat_axis=0, tiled=True)
    return jnp.sum(arrived.astype(jnp.float32), axis=0)


def per_device(queries, documents, candidates):
    local_docs, doc_len, width = documents.shape
    per_group, query_len, _ = queries.shape
    slots = candidates.shape[1]
    rows_of_y = lax.axis_size("y")
    groups = lax.axis_size(QG)
    total_queries = per_group * groups
    half_rows = total_queries * query_len // 2
    core = lax.axis_index("c")

    own = copy_for_each(queries, "y").reshape(half_rows, width)
    halves = [own, other_core(own)]

    def scored(rows):
        return sharpness_factor * lax.dot_general(
            rows, documents, (((1,), (2,)), ((), ())), preferred_element_type=jnp.float32
        )

    local_lse = []
    for rows in halves:
        part = scored(rows)
        peak = jnp.max(part, axis=2)
        mass = jnp.sum(jnp.exp(part - peak[:, :, None]), axis=2)
        local_lse.append(peak + jnp.log(mass))

    own_order = jnp.concatenate(local_lse).T.reshape(local_docs, 2, -1, 128)
    lse = jnp.where(core == 0, own_order, own_order[:, ::-1]).reshape(-1, 128)
    lse = log_of_sum(copy_for_each(lse, ("h", "l")))
    everyone = copy_for_each(lse, ("x", *QG))
    lse = log_of_sum(everyone.reshape(lax.axis_size("x"), -1, 128))
    lse, candidates, core, group = lax.optimization_barrier(
        (lse, candidates, core, lax.axis_index(QG))
    )

    all_docs = groups * local_docs
    scores = jnp.sum(lse.reshape(all_docs, total_queries, query_len), axis=2) / sharpness_factor
    by_core = candidates.reshape(rows_of_y, 2, per_group, slots).swapaxes(0, 1)
    by_core = by_core.reshape(total_queries, slots)
    picks = by_core[:, :, None] == jnp.arange(all_docs, dtype=jnp.int32)[None, None, :]
    pair = jnp.sum(jnp.where(picks, scores.T[:, None, :], 0.0), axis=2)
    highest = jnp.max(pair, axis=1, keepdims=True)
    total = highest + jnp.log(jnp.sum(jnp.exp(pair - highest), axis=1, keepdims=True))
    first = lax.broadcasted_iota(jnp.int32, pair.shape, 1) == 0
    dz = loss_scale / total_queries * (jnp.exp(pair - total) - jnp.where(first, 1.0, 0.0))
    owned = by_core[:, :, None] - group * local_docs == jnp.arange(local_docs, dtype=jnp.int32)
    weights = jnp.sum(jnp.where(owned, dz[:, :, None], 0.0), axis=1).reshape(2, -1, local_docs)
    weights = jnp.where(core == 0, weights, weights[::-1]).reshape(total_queries, local_docs)
    row_weight = jnp.repeat(weights, query_len, axis=0)
    mine = lax.dynamic_slice_in_dim(lse, group * len(own_order.reshape(-1, 128)), len(lse) // groups)
    mine = mine.reshape(own_order.shape)
    norm = jnp.where(core == 0, mine, mine[:, ::-1]).reshape(local_docs, -1).T

    def weighted_half(k):
        at = slice(k * half_rows, (k + 1) * half_rows)
        rows, this_norm, this_weight = lax.optimization_barrier(
            (halves[k], norm[at], row_weight[at])
        )
        prob = jnp.exp(scored(rows) - this_norm[:, :, None])
        return lax.optimization_barrier((this_weight[:, :, None] * prob).astype(jnp.bfloat16))

    def grad_of_rows(weighted):
        return lax.dot_general(
            weighted, documents, (((1, 2), (0, 1)), ((), ())), preferred_element_type=jnp.float32
        )

    theirs = weighted_half(1)
    received = other_core(grad_of_rows(theirs).astype(jnp.bfloat16))
    ours = weighted_half(0)
    chip = lax.optimization_barrier(grad_of_rows(ours)) + received.astype(jnp.float32)
    summed = sent_and_summed(chip, ("y", "x"))
    near = summed.astype(jnp.bfloat16).reshape(lax.axis_size("l"), -1, width)
    tiles = jnp.broadcast_to(near, (lax.axis_size("h"), *near.shape)).reshape(-1, *near.shape[1:])
    arrived = lax.all_to_all(tiles, ("h", "l"), split_axis=0, concat_axis=0, tiled=True)
    part = jnp.sum(arrived.astype(jnp.float32), axis=0).astype(jnp.bfloat16)
    part, total, pair = lax.optimization_barrier((part, total, pair))
    loss = jnp.mean(total - pair[:, :1])
    grad_q = copy_for_each(part, ("x", "l")).reshape(queries.shape)
    grad_docs = sum(
        lax.dot_general(w, rows, (((0,), (0,)), ((), ())), preferred_element_type=jnp.float32)
        for w, rows in zip((ours, theirs), halves)
    ).astype(jnp.bfloat16)
    return loss, grad_q, grad_docs


def solution(mesh):
    finer = Mesh(mesh.devices.reshape(4, 4, 4, 4, 2), ("x", "h", "l", "y", "c"))
    in_specs = (P(QG, None, None), P(QG, CTX, None), P())
    out_specs = (P(), P(QG, None, None), P(QG, CTX, None))
    return jax.shard_map(
        per_device, mesh=finer, in_specs=in_specs, out_specs=out_specs, check_vma=False
    )
```

```python
import jax
import jax.numpy as jnp
from jax import lax
from jax.sharding import Mesh
from jax.sharding import PartitionSpec as P

QG = ("y", "c")
CTX = ("x", "h", "m", "p")

sharpness_factor = 2.0
loss_scale = 1024.0


def copy_for_each(x, axis):
    copies = jnp.broadcast_to(x, (lax.axis_size(axis), *x.shape))
    return lax.all_to_all(copies, axis, split_axis=0, concat_axis=0, tiled=True)


def shared_and_scattered(x, far, near):
    tiles = x.reshape(lax.axis_size(near), -1, x.shape[-1])
    copies = jnp.broadcast_to(tiles, (lax.axis_size(far), *tiles.shape))
    copies = copies.reshape(-1, *tiles.shape[1:])
    return lax.all_to_all(copies, (*far, near), split_axis=0, concat_axis=0, tiled=True)


def other_core(x):
    return lax.ppermute(x, "c", [(0, 1), (1, 0)])


def log_of_sum(x):
    top = jnp.max(x, axis=0)
    return top + jnp.log(jnp.sum(jnp.exp(x - top[None]), axis=0))


def sent_and_summed(x, axis):
    tiles = x.astype(jnp.bfloat16).reshape(lax.axis_size(axis), -1, x.shape[-1])
    arrived = lax.all_to_all(tiles, axis, split_axis=0, concat_axis=0, tiled=True)
    return jnp.sum(arrived.astype(jnp.float32), axis=0)


def per_device(queries, documents, candidates):
    local_docs, doc_len, width = documents.shape
    per_group, query_len, _ = queries.shape
    slots = candidates.shape[1]
    rows_of_y = lax.axis_size("y")
    groups = lax.axis_size(QG)
    total_queries = per_group * groups
    half_rows = total_queries * query_len // 2
    core = lax.axis_index("c")

    own = copy_for_each(queries, "y").reshape(half_rows, width)
    halves = [own, other_core(own)]

    def scored(rows):
        return sharpness_factor * lax.dot_general(
            rows, documents, (((1,), (2,)), ((), ())), preferred_element_type=jnp.float32
        )

    local_lse = []
    for rows in halves:
        part = scored(rows)
        peak = jnp.max(part, axis=2)
        mass = jnp.sum(jnp.exp(part - peak[:, :, None]), axis=2)
        local_lse.append(peak + jnp.log(mass))

    own_order = jnp.concatenate(local_lse).T.reshape(local_docs, 2, -1, 128)
    lse = jnp.where(core == 0, own_order, own_order[:, ::-1]).reshape(-1, 128)
    lse = log_of_sum(shared_and_scattered(lse, ("h", "m"), "p"))
    everyone = copy_for_each(lse, ("x", *QG, "p"))
    lse = log_of_sum(everyone.reshape(lax.axis_size("x"), -1, 128))
    lse, candidates, core, group = lax.optimization_barrier(
        (lse, candidates, core, lax.axis_index(QG))
    )

    all_docs = groups * local_docs
    scores = jnp.sum(lse.reshape(all_docs, total_queries, query_len), axis=2) / sharpness_factor
    by_core = candidates.reshape(rows_of_y, 2, per_group, slots).swapaxes(0, 1)
    by_core = by_core.reshape(total_queries, slots)
    picks = by_core[:, :, None] == jnp.arange(all_docs, dtype=jnp.int32)[None, None, :]
    pair = jnp.sum(jnp.where(picks, scores.T[:, None, :], 0.0), axis=2)
    highest = jnp.max(pair, axis=1, keepdims=True)
    total = highest + jnp.log(jnp.sum(jnp.exp(pair - highest), axis=1, keepdims=True))
    first = lax.broadcasted_iota(jnp.int32, pair.shape, 1) == 0
    dz = loss_scale / total_queries * (jnp.exp(pair - total) - jnp.where(first, 1.0, 0.0))
    owned = by_core[:, :, None] - group * local_docs == jnp.arange(local_docs, dtype=jnp.int32)
    weights = jnp.sum(jnp.where(owned, dz[:, :, None], 0.0), axis=1).reshape(2, -1, local_docs)
    weights = jnp.where(core == 0, weights, weights[::-1]).reshape(total_queries, local_docs)
    row_weight = jnp.repeat(weights, query_len, axis=0)
    mine = lax.dynamic_slice_in_dim(lse, group * len(own_order.reshape(-1, 128)), len(lse) // groups)
    mine = mine.reshape(own_order.shape)
    norm = jnp.where(core == 0, mine, mine[:, ::-1]).reshape(local_docs, -1).T

    def weighted_half(k):
        at = slice(k * half_rows, (k + 1) * half_rows)
        rows, this_norm, this_weight = lax.optimization_barrier(
            (halves[k], norm[at], row_weight[at])
        )
        prob = jnp.exp(scored(rows) - this_norm[:, :, None])
        return lax.optimization_barrier((this_weight[:, :, None] * prob).astype(jnp.bfloat16))

    def grad_of_rows(weighted):
        return lax.dot_general(
            weighted, documents, (((1, 2), (0, 1)), ((), ())), preferred_element_type=jnp.float32
        )

    theirs = weighted_half(1)
    received = other_core(grad_of_rows(theirs).astype(jnp.bfloat16))
    ours = weighted_half(0)
    chip = lax.optimization_barrier(grad_of_rows(ours)) + received.astype(jnp.float32)
    summed = sent_and_summed(chip, ("y", "x", "p"))
    arrived = shared_and_scattered(summed.astype(jnp.bfloat16), ("h",), "m")
    part = jnp.sum(arrived.astype(jnp.float32), axis=0).astype(jnp.bfloat16)
    part, total, pair = lax.optimization_barrier((part, total, pair))
    loss = jnp.mean(total - pair[:, :1])
    grad_q = copy_for_each(part, ("x", "p", "m")).reshape(queries.shape)
    grad_docs = sum(
        lax.dot_general(w, rows, (((0,), (0,)), ((), ())), preferred_element_type=jnp.float32)
        for w, rows in zip((ours, theirs), halves)
    ).astype(jnp.bfloat16)
    return loss, grad_q, grad_docs


def solution(mesh):
    finer = Mesh(mesh.devices.reshape(4, 4, 2, 2, 4, 2), ("x", "h", "m", "p", "y", "c"))
    in_specs = (P(QG, None, None), P(QG, CTX, None), P())
    out_specs = (P(), P(QG, None, None), P(QG, CTX, None))
    return jax.shard_map(
        per_device, mesh=finer, in_specs=in_specs, out_specs=out_specs, check_vma=False
    )
```

```python
import jax
import jax.numpy as jnp
from jax import lax
from jax.sharding import Mesh
from jax.sharding import PartitionSpec as P

QG = ("y", "c")
CTX = ("x", "h", "m", "p")

sharpness_factor = 2.0
loss_scale = 1024.0


def copy_for_each(x, axis):
    copies = jnp.broadcast_to(x, (lax.axis_size(axis), *x.shape))
    return lax.all_to_all(copies, axis, split_axis=0, concat_axis=0, tiled=True)


def shared_and_scattered(x, far, near):
    tiles = x.reshape(lax.axis_size(near), -1, x.shape[-1])
    copies = jnp.broadcast_to(tiles, (lax.axis_size(far), *tiles.shape))
    copies = copies.reshape(-1, *tiles.shape[1:])
    return lax.all_to_all(copies, (*far, near), split_axis=0, concat_axis=0, tiled=True)


def other_core(x):
    return lax.ppermute(x, "c", [(0, 1), (1, 0)])


def log_of_sum(x):
    top = jnp.max(x, axis=0)
    return top + jnp.log(jnp.sum(jnp.exp(x - top[None]), axis=0))


def sent_and_summed(x, axis):
    tiles = x.astype(jnp.bfloat16).reshape(lax.axis_size(axis), -1, x.shape[-1])
    arrived = lax.all_to_all(tiles, axis, split_axis=0, concat_axis=0, tiled=True)
    return jnp.sum(arrived.astype(jnp.float32), axis=0)


def per_device(queries, documents, candidates):
    local_docs, doc_len, width = documents.shape
    per_group, query_len, _ = queries.shape
    slots = candidates.shape[1]
    rows_of_y = lax.axis_size("y")
    groups = lax.axis_size(QG)
    total_queries = per_group * groups
    half_rows = total_queries * query_len // 2
    core = lax.axis_index("c")

    own = copy_for_each(queries, "y").reshape(half_rows, width)
    halves = [own, other_core(own)]

    def scored(rows):
        return sharpness_factor * lax.dot_general(
            rows, documents, (((1,), (2,)), ((), ())), preferred_element_type=jnp.float32
        )

    local_lse = []
    for rows in halves:
        part = scored(rows)
        peak = jnp.max(part, axis=2)
        mass = jnp.sum(jnp.exp(part - peak[:, :, None]), axis=2)
        local_lse.append(peak + jnp.log(mass))

    own_order = jnp.concatenate(local_lse).T.reshape(local_docs, 2, -1, 128)
    lse = jnp.where(core == 0, own_order, own_order[:, ::-1]).reshape(-1, 128)
    group = lax.axis_index(QG)
    by_core = candidates.reshape(rows_of_y, 2, per_group, slots).swapaxes(0, 1)
    by_core = by_core.reshape(total_queries, slots)
    place = (group * local_docs, group * own_order.size // 128, core, by_core)
    lse, place = lax.optimization_barrier((lse, place))
    lse = log_of_sum(shared_and_scattered(lse, ("h", "m"), "p"))
    everyone = copy_for_each(lse, ("x", *QG, "p"))
    everyone, place = lax.optimization_barrier((everyone, place))
    first_doc, first_row, core, by_core = place
    lse = log_of_sum(everyone.reshape(lax.axis_size("x"), -1, 128))

    all_docs = groups * local_docs
    scores = jnp.sum(lse.reshape(all_docs, total_queries, query_len), axis=2) / sharpness_factor
    picks = by_core[:, :, None] == jnp.arange(all_docs, dtype=jnp.int32)[None, None, :]
    pair = jnp.sum(jnp.where(picks, scores.T[:, None, :], 0.0), axis=2)
    highest = jnp.max(pair, axis=1, keepdims=True)
    total = highest + jnp.log(jnp.sum(jnp.exp(pair - highest), axis=1, keepdims=True))
    first = lax.broadcasted_iota(jnp.int32, pair.shape, 1) == jnp.minimum(first_doc, 0)
    dz = loss_scale / total_queries * (jnp.exp(pair - total) - jnp.where(first, 1.0, 0.0))
    owned = by_core[:, :, None] - first_doc == jnp.arange(local_docs, dtype=jnp.int32)
    weights = jnp.sum(jnp.where(owned, dz[:, :, None], 0.0), axis=1).reshape(2, -1, local_docs)
    weights = jnp.where(core == 0, weights, weights[::-1]).reshape(total_queries, local_docs)
    row_weight = jnp.repeat(weights, query_len, axis=0)
    mine = lax.dynamic_slice_in_dim(lse, first_row, own_order.size // 128)
    mine = mine.reshape(own_order.shape)
    norm = jnp.where(core == 0, mine, mine[:, ::-1]).reshape(local_docs, -1).T

    def weighted_half(k):
        at = slice(k * half_rows, (k + 1) * half_rows)
        rows, this_norm, this_weight = lax.optimization_barrier(
            (halves[k], norm[at], row_weight[at])
        )
        prob = jnp.exp(scored(rows) - this_norm[:, :, None])
        return lax.optimization_barrier((this_weight[:, :, None] * prob).astype(jnp.bfloat16))

    def grad_of_rows(weighted):
        return lax.dot_general(
            weighted, documents, (((1, 2), (0, 1)), ((), ())), preferred_element_type=jnp.float32
        )

    theirs = weighted_half(1)
    received = other_core(grad_of_rows(theirs).astype(jnp.bfloat16))
    ours = weighted_half(0)
    chip = lax.optimization_barrier(grad_of_rows(ours)) + received.astype(jnp.float32)
    summed = sent_and_summed(chip, ("y", "x", "p"))
    arrived = shared_and_scattered(summed.astype(jnp.bfloat16), ("h",), "m")
    part = jnp.sum(arrived.astype(jnp.float32), axis=0).astype(jnp.bfloat16)
    part, total, pair = lax.optimization_barrier((part, total, pair))
    loss = jnp.mean(total - pair[:, :1])
    grad_q = copy_for_each(part, ("x", "p", "m")).reshape(queries.shape)
    grad_docs = sum(
        lax.dot_general(w, rows, (((0,), (0,)), ((), ())), preferred_element_type=jnp.float32)
        for w, rows in zip((ours, theirs), halves)
    ).astype(jnp.bfloat16)
    return loss, grad_q, grad_docs


def solution(mesh):
    finer = Mesh(mesh.devices.reshape(4, 4, 2, 2, 4, 2), ("x", "h", "m", "p", "y", "c"))
    in_specs = (P(QG, None, None), P(QG, CTX, None), P())
    out_specs = (P(), P(QG, None, None), P(QG, CTX, None))
    return jax.shard_map(
        per_device, mesh=finer, in_specs=in_specs, out_specs=out_specs, check_vma=False
    )
```

```python
import jax
import jax.numpy as jnp
from jax import lax
from jax.sharding import Mesh
from jax.sharding import PartitionSpec as P

QG = ("y", "c")
CTX = ("x", "h", "m", "p")

sharpness_factor = 2.0
loss_scale = 1024.0


def copy_for_each(x, axis):
    copies = jnp.broadcast_to(x, (lax.axis_size(axis), *x.shape))
    return lax.all_to_all(copies, axis, split_axis=0, concat_axis=0, tiled=True)


def shared_and_scattered(x, far, near):
    tiles = x.reshape(lax.axis_size(near), -1, x.shape[-1])
    copies = jnp.broadcast_to(tiles, (lax.axis_size(far), *tiles.shape))
    copies = copies.reshape(-1, *tiles.shape[1:])
    return lax.all_to_all(copies, (*far, near), split_axis=0, concat_axis=0, tiled=True)


def other_core(x):
    return lax.ppermute(x, "c", [(0, 1), (1, 0)])


def log_of_sum(x):
    top = jnp.max(x, axis=0)
    return top + jnp.log(jnp.sum(jnp.exp(x - top[None]), axis=0))


def sent_and_summed(x, axis):
    tiles = x.astype(jnp.bfloat16).reshape(lax.axis_size(axis), -1, x.shape[-1])
    arrived = lax.all_to_all(tiles, axis, split_axis=0, concat_axis=0, tiled=True)
    return jnp.sum(arrived.astype(jnp.float32), axis=0)


def per_device(queries, documents, candidates):
    local_docs, doc_len, width = documents.shape
    per_group, query_len, _ = queries.shape
    slots = candidates.shape[1]
    rows_of_y = lax.axis_size("y")
    groups = lax.axis_size(QG)
    total_queries = per_group * groups
    half_rows = total_queries * query_len // 2
    core = lax.axis_index("c")

    own = copy_for_each(queries, "y").reshape(half_rows, width)
    halves = [own, other_core(own)]

    def scored(rows):
        return sharpness_factor * lax.dot_general(
            rows, documents, (((1,), (2,)), ((), ())), preferred_element_type=jnp.float32
        )

    local_lse = []
    for rows in halves:
        part = scored(rows)
        peak = jnp.max(part, axis=2)
        mass = jnp.sum(jnp.exp(part - peak[:, :, None]), axis=2)
        local_lse.append(peak + jnp.log(mass))

    own_order = jnp.concatenate(local_lse).T.reshape(local_docs, 2, -1, 128)
    lse = jnp.where(core == 0, own_order, own_order[:, ::-1]).reshape(-1, 128)
    group = lax.axis_index(QG)
    by_core = candidates.reshape(rows_of_y, 2, per_group, slots).swapaxes(0, 1)
    by_core = by_core.reshape(total_queries, slots)
    place = (group * local_docs, group * own_order.size // 128, core, by_core)
    lse, place = lax.optimization_barrier((lse, place))
    lse = log_of_sum(shared_and_scattered(lse, ("h", "m"), "p"))
    everyone = copy_for_each(lse, (*QG, "x", "p"))
    everyone, place = lax.optimization_barrier((everyone, place))
    first_doc, first_row, core, by_core = place
    lse = log_of_sum(everyone.reshape(groups, lax.axis_size("x"), -1, 128).swapaxes(0, 1)).reshape(-1, 128)

    all_docs = groups * local_docs
    scores = jnp.sum(lse.reshape(all_docs, total_queries, query_len), axis=2) / sharpness_factor
    picks = by_core[:, :, None] == jnp.arange(all_docs, dtype=jnp.int32)[None, None, :]
    pair = jnp.sum(jnp.where(picks, scores.T[:, None, :], 0.0), axis=2)
    highest = jnp.max(pair, axis=1, keepdims=True)
    total = highest + jnp.log(jnp.sum(jnp.exp(pair - highest), axis=1, keepdims=True))
    first = lax.broadcasted_iota(jnp.int32, pair.shape, 1) == jnp.minimum(first_doc, 0)
    dz = loss_scale / total_queries * (jnp.exp(pair - total) - jnp.where(first, 1.0, 0.0))
    owned = by_core[:, :, None] - first_doc == jnp.arange(local_docs, dtype=jnp.int32)
    weights = jnp.sum(jnp.where(owned, dz[:, :, None], 0.0), axis=1).reshape(2, -1, local_docs)
    weights = jnp.where(core == 0, weights, weights[::-1]).reshape(total_queries, local_docs)
    row_weight = jnp.repeat(weights, query_len, axis=0)
    mine = lax.dynamic_slice_in_dim(lse, first_row, own_order.size // 128)
    mine = mine.reshape(own_order.shape)
    norm = jnp.where(core == 0, mine, mine[:, ::-1]).reshape(local_docs, -1).T

    def weighted_half(k):
        at = slice(k * half_rows, (k + 1) * half_rows)
        rows, this_norm, this_weight = lax.optimization_barrier(
            (halves[k], norm[at], row_weight[at])
        )
        prob = jnp.exp(scored(rows) - this_norm[:, :, None])
        return lax.optimization_barrier((this_weight[:, :, None] * prob).astype(jnp.bfloat16))

    def grad_of_rows(weighted):
        return lax.dot_general(
            weighted, documents, (((1, 2), (0, 1)), ((), ())), preferred_element_type=jnp.float32
        )

    theirs = weighted_half(1)
    received = other_core(grad_of_rows(theirs).astype(jnp.bfloat16))
    ours = weighted_half(0)
    chip = lax.optimization_barrier(grad_of_rows(ours)) + received.astype(jnp.float32)
    summed = sent_and_summed(chip, ("y", "x", "p"))
    arrived = shared_and_scattered(summed.astype(jnp.bfloat16), ("h",), "m")
    part = jnp.sum(arrived.astype(jnp.float32), axis=0).astype(jnp.bfloat16)
    part, total, pair = lax.optimization_barrier((part, total, pair))
    loss = jnp.mean(total - pair[:, :1])
    grad_q = copy_for_each(part, ("x", "p", "m")).reshape(queries.shape)
    grad_docs = sum(
        lax.dot_general(w, rows, (((0,), (0,)), ((), ())), preferred_element_type=jnp.float32)
        for w, rows in zip((ours, theirs), halves)
    ).astype(jnp.bfloat16)
    return loss, grad_q, grad_docs


def solution(mesh):
    finer = Mesh(mesh.devices.reshape(4, 4, 2, 2, 4, 2), ("x", "h", "m", "p", "y", "c"))
    in_specs = (P(QG, None, None), P(QG, CTX, None), P())
    out_specs = (P(), P(QG, None, None), P(QG, CTX, None))
    return jax.shard_map(
        per_device, mesh=finer, in_specs=in_specs, out_specs=out_specs, check_vma=False
    )
```

```python
import jax
import jax.numpy as jnp
from jax import lax
from jax.sharding import Mesh
from jax.sharding import PartitionSpec as P

QG = ("y", "c")
CTX = ("x", "h", "m", "p")

sharpness_factor = 2.0
loss_scale = 1024.0


def copy_for_each(x, axis):
    copies = jnp.broadcast_to(x, (lax.axis_size(axis), *x.shape))
    return lax.all_to_all(copies, axis, split_axis=0, concat_axis=0, tiled=True)


def shared_and_scattered(x, far, near):
    tiles = x.reshape(lax.axis_size(near), -1, x.shape[-1])
    copies = jnp.repeat(tiles, lax.axis_size(far), axis=0)
    return lax.all_to_all(copies, (near, *far), split_axis=0, concat_axis=0, tiled=True)


def other_core(x):
    return lax.ppermute(x, "c", [(0, 1), (1, 0)])


def log_of_sum(x):
    top = jnp.max(x, axis=0)
    return top + jnp.log(jnp.sum(jnp.exp(x - top[None]), axis=0))


def sent_and_summed(x, axis):
    tiles = x.astype(jnp.bfloat16).reshape(lax.axis_size(axis), -1, x.shape[-1])
    arrived = lax.all_to_all(tiles, axis, split_axis=0, concat_axis=0, tiled=True)
    return jnp.sum(arrived.astype(jnp.float32), axis=0)


def per_device(queries, documents, candidates):
    local_docs, doc_len, width = documents.shape
    per_group, query_len, _ = queries.shape
    slots = candidates.shape[1]
    rows_of_y = lax.axis_size("y")
    groups = lax.axis_size(QG)
    total_queries = per_group * groups
    half_rows = total_queries * query_len // 2
    core = lax.axis_index("c")

    own = copy_for_each(queries, "y").reshape(half_rows, width)
    halves = [own, other_core(own)]

    def scored(rows):
        return sharpness_factor * lax.dot_general(
            rows, documents, (((1,), (2,)), ((), ())), preferred_element_type=jnp.float32
        )

    local_lse = []
    for rows in halves:
        part = scored(rows)
        peak = jnp.max(part, axis=2)
        mass = jnp.sum(jnp.exp(part - peak[:, :, None]), axis=2)
        local_lse.append(peak + jnp.log(mass))

    own_order = jnp.concatenate(local_lse).T.reshape(local_docs, 2, -1, 128)
    lse = jnp.where(core == 0, own_order, own_order[:, ::-1]).reshape(-1, 128)
    group = lax.axis_index(QG)
    by_core = candidates.reshape(rows_of_y, 2, per_group, slots).swapaxes(0, 1)
    by_core = by_core.reshape(total_queries, slots)
    place = (group * local_docs, group * own_order.size // 128, core, by_core)
    lse, place = lax.optimization_barrier((lse, place))
    lse = log_of_sum(shared_and_scattered(lse, ("h", "m"), "p"))
    everyone = copy_for_each(lse, (*QG, "x", "p"))
    everyone, place = lax.optimization_barrier((everyone, place))
    first_doc, first_row, core, by_core = place
    lse = log_of_sum(everyone.reshape(groups, lax.axis_size("x"), -1, 128).swapaxes(0, 1)).reshape(-1, 128)

    all_docs = groups * local_docs
    scores = jnp.sum(lse.reshape(all_docs, total_queries, query_len), axis=2) / sharpness_factor
    picks = by_core[:, :, None] == jnp.arange(all_docs, dtype=jnp.int32)[None, None, :]
    pair = jnp.sum(jnp.where(picks, scores.T[:, None, :], 0.0), axis=2)
    highest = jnp.max(pair, axis=1, keepdims=True)
    total = highest + jnp.log(jnp.sum(jnp.exp(pair - highest), axis=1, keepdims=True))
    first = lax.broadcasted_iota(jnp.int32, pair.shape, 1) == jnp.minimum(first_doc, 0)
    dz = loss_scale / total_queries * (jnp.exp(pair - total) - jnp.where(first, 1.0, 0.0))
    owned = by_core[:, :, None] - first_doc == jnp.arange(local_docs, dtype=jnp.int32)
    weights = jnp.sum(jnp.where(owned, dz[:, :, None], 0.0), axis=1).reshape(2, -1, local_docs)
    weights = jnp.where(core == 0, weights, weights[::-1]).reshape(total_queries, local_docs)
    row_weight = jnp.repeat(weights, query_len, axis=0)
    mine = lax.dynamic_slice_in_dim(lse, first_row, own_order.size // 128)
    mine = mine.reshape(own_order.shape)
    norm = jnp.where(core == 0, mine, mine[:, ::-1]).reshape(local_docs, -1).T

    def weighted_half(k):
        at = slice(k * half_rows, (k + 1) * half_rows)
        rows, this_norm, this_weight = lax.optimization_barrier(
            (halves[k], norm[at], row_weight[at])
        )
        prob = jnp.exp(scored(rows) - this_norm[:, :, None])
        return lax.optimization_barrier((this_weight[:, :, None] * prob).astype(jnp.bfloat16))

    def grad_of_rows(weighted):
        return lax.dot_general(
            weighted, documents, (((1, 2), (0, 1)), ((), ())), preferred_element_type=jnp.float32
        )

    theirs = weighted_half(1)
    received = other_core(grad_of_rows(theirs).astype(jnp.bfloat16))
    ours = weighted_half(0)
    chip = lax.optimization_barrier(grad_of_rows(ours)) + received.astype(jnp.float32)
    summed = sent_and_summed(chip, ("y", "x", "p"))
    arrived = shared_and_scattered(summed.astype(jnp.bfloat16), ("h",), "m")
    part = jnp.sum(arrived.astype(jnp.float32), axis=0).astype(jnp.bfloat16)
    part, total, pair = lax.optimization_barrier((part, total, pair))
    loss = jnp.mean(total - pair[:, :1])
    grad_q = copy_for_each(part, ("x", "p", "m")).reshape(queries.shape)
    grad_docs = sum(
        lax.dot_general(w, rows, (((0,), (0,)), ((), ())), preferred_element_type=jnp.float32)
        for w, rows in zip((ours, theirs), halves)
    ).astype(jnp.bfloat16)
    return loss, grad_q, grad_docs


def solution(mesh):
    finer = Mesh(mesh.devices.reshape(4, 4, 2, 2, 4, 2), ("x", "h", "m", "p", "y", "c"))
    in_specs = (P(QG, None, None), P(QG, CTX, None), P())
    out_specs = (P(), P(QG, None, None), P(QG, CTX, None))
    return jax.shard_map(
        per_device, mesh=finer, in_specs=in_specs, out_specs=out_specs, check_vma=False
    )
```
